32 devices in a mesh: ctx: 16 (over z, y, core), head: 2 (over x).
Axes of the slice: x: 2, y: 2, z: 4, core: 2. Of those that a mesh axis runs over, the one named last changes fastest.
Arguments:
- fine_query: bfloat16 [4096, 4096], P('ctx', 'head'), may hold values from -181 to 181
- fine_memory: bfloat16 [2, 4096, 1024], P(None, 'ctx', 'head'), may hold values from -6.5 to 6.5
- coarse_query: bfloat16 [2048, 4096], P('ctx', 'head'), may hold values from -181 to 181
- coarse_memory: bfloat16 [2, 2048, 1024], P(None, 'ctx', 'head'), may hold values from -6.5 to 6.5
- coarse_scale: int32 [2048], P('ctx'), may hold values from 0 to 7, never falling along the last dimension, each value on 1 to 512 neighbouring positions
- out_weight: bfloat16 [4096, 4096], P('head'), may hold values from -0.09375 to 0.09375
Outputs:
- fine_mixed: bfloat16 [4096, 4096], P(('ctx', 'head'))
- coarse_mixed: bfloat16 [2048, 4096], P(('ctx', 'head'))
The draws below stay inside these ranges and needn't reach their ends.
Inputs may be any that keep to these rules, and one draw needn't show every extreme that they name: `coarse_scale`: never falls along the coarse tokens.
All inputs are finite; a program needn't handle non-finite values.
Results may differ from the reference program's by a relative error of at most 0.014.
Values may be sent and summed in bfloat16 or wider, within the bound.
A program may use at most 128 MiB of HBM per device.

```python
import math
import jax
import jax.numpy as jnp
import numpy as np
from jax import lax

D = 4096
QH = 32
KVH = 8
HD = 128
SCALES = 8
FINE = 4096
COARSE = 2048


def drawn_keys(key, length, width, salt):
    base = jax.random.truncated_normal(jax.random.fold_in(key, salt), -6.0, 6.0, (length, width), jnp.float32)
    return base


def drawn_queries(key, length, salt_query):
    query = 2.5 * jax.random.truncated_normal(jax.random.fold_in(key, salt_query), -6.0, 6.0, (length, QH * HD), jnp.float32)
    return query


def memory_pair(key, length, salt_keys, salt_values):
    keyset = drawn_keys(key, length, KVH * HD, salt_keys)
    valueset = jax.random.truncated_normal(jax.random.fold_in(key, salt_values), -6.0, 6.0, (length, KVH * HD), jnp.float32)
    return jnp.stack([keyset, valueset]).astype(jnp.bfloat16)


def draw_fine_query(key, part):
    return drawn_queries(key, FINE, 17).astype(jnp.bfloat16)


def draw_fine_memory(key, part):
    return memory_pair(key, FINE, 11, 13)


def draw_coarse_query(key, part):
    return drawn_queries(key, COARSE, 27).astype(jnp.bfloat16)


def draw_coarse_memory(key, part):
    return memory_pair(key, COARSE, 21, 23)


def steps_of(key, extent, split, smallest, largest):
    loudness = 1.0
    for axis_at, blocks in split:
        steps = jax.random.uniform(jax.random.fold_in(jax.random.fold_in(key, 6), axis_at), (blocks,), jnp.float32, smallest / len(split), largest / len(split))
        loudness = loudness * jnp.repeat(jnp.exp(steps), extent[axis_at] // blocks).reshape((-1,) + (1,) * (len(extent) - 1 - axis_at))
    return loudness


def length_profile(count, total, most, lean):
    weights = [(1 << 20) // math.isqrt(rank ** lean) + 1 for rank in range(2, count + 1)]
    surplus, given = total - most - (count - 1), [1] * (count - 1)
    while surplus > 0:
        candidates = [i for i in range(count - 1) if given[i] < most]
        mass, left = sum([weights[i] for i in candidates]), surplus
        for i in candidates:
            extra = min(most - given[i], max(1, left * weights[i] // mass), surplus)
            given[i] = given[i] + extra
            surplus = surplus - extra
    return np.array([most] + given)


def ragged(rng, amount, total, limit, slope):
    if amount == 2:
        one = jax.random.randint(rng, (), max(1, total - limit), min(limit, total - 1) + 1)
        return jnp.stack([one, total - one])
    tallies = jnp.asarray(length_profile(amount, total, limit, slope), jnp.int32)
    couples = (amount - 1) // 2
    source_of, receiver = tallies[1:1 + 2 * couples:2], tallies[2:2 + 2 * couples:2]
    slack = jnp.minimum(source_of - 1, limit - receiver)
    moved = jax.random.randint(jax.random.fold_in(rng, 1), (couples,), 0, 1 << 20) % (slack + 1)
    tallies = tallies.at[1:1 + 2 * couples:2].set(source_of - moved).at[2:2 + 2 * couples:2].set(receiver + moved)
    return tallies[jax.random.permutation(jax.random.fold_in(rng, 2), amount)]


def centred(rng, dims, scale, limit, split=(), dtype=jnp.bfloat16):
    values = jax.random.normal(rng, dims, jnp.float32) * scale
    if len(split) > 0:
        values = steps_of(rng, dims, split, -0.22, 0.18) * values
    return jnp.clip(values, min=-limit, max=limit).astype(dtype)


def setup_inputs(seed: int = 0) -> dict:
    key_of = jax.random.split(jax.random.key(seed), 7)
    fine_query = draw_fine_query(jax.random.fold_in(key_of[6], 71), 0)
    fine_memory = draw_fine_memory(jax.random.fold_in(key_of[6], 71), 0)
    coarse_query = draw_coarse_query(jax.random.fold_in(key_of[6], 71), 0)
    coarse_memory = draw_coarse_memory(jax.random.fold_in(key_of[6], 71), 0)
    coarse_scale = jnp.searchsorted(jnp.cumsum(ragged(key_of[4], SCALES, COARSE, COARSE // 4, 1)), jnp.arange(COARSE), side="right").astype(jnp.int32)
    out_weight = centred(key_of[5], (QH * HD, D), (QH * HD) ** -0.5, 0.09375, ((0, 2),))
    return {"fine_query": fine_query, "fine_memory": fine_memory, "coarse_query": coarse_query, "coarse_memory": coarse_memory, "coarse_scale": coarse_scale, "out_weight": out_weight}


masked_score = -1e30


def attend(queries, key_rows, value_rows, q_level, k_level):
    length = queries.shape[0]
    grouped = queries.astype(jnp.float32).reshape(length, KVH, QH // KVH, HD)
    key_heads = key_rows.astype(jnp.float32).reshape(-1, KVH, HD)
    value_heads = value_rows.astype(jnp.float32).reshape(-1, KVH, HD)
    scores = jnp.einsum('rkgd,skd->kgrs', grouped, key_heads) * (HD ** -0.5)
    allowed = k_level[None, :] <= q_level[:, None]
    scores = jnp.where(allowed[None, None], scores, masked_score)
    highest = jnp.max(scores, axis=-1, keepdims=True)
    shifted = jnp.exp(scores - highest)
    totals = jnp.sum(shifted, axis=-1)
    weights = lax.optimization_barrier(shifted.astype(jnp.bfloat16)).astype(jnp.float32)
    result = jnp.einsum('kgrs,skd->kgrd', weights, value_heads) / totals[..., None]
    return result.transpose(2, 0, 1, 3).reshape(length, QH * HD).astype(jnp.bfloat16)


def run_rows(queries, q_level, key_rows, value_rows, k_level):
    width = queries.shape[1]
    query_blocks = queries.reshape(-1, 64, width)
    level_blocks = q_level.reshape(-1, 64)
    mapped = lax.map(lambda pair: attend(pair[0], key_rows, value_rows, pair[1], k_level), (query_blocks, level_blocks))
    return mapped.reshape(-1, width)


def reference(fine_query, fine_memory, coarse_query, coarse_memory, coarse_scale, out_weight):
    fine_level = jnp.full((FINE,), SCALES, jnp.int32)
    all_keys = jnp.concatenate([fine_memory[0], coarse_memory[0]], axis=0)
    all_values = jnp.concatenate([fine_memory[1], coarse_memory[1]], axis=0)
    all_levels = jnp.concatenate([fine_level, coarse_scale.astype(jnp.int32)], axis=0)
    fine_attention = run_rows(fine_query, fine_level, all_keys, all_values, all_levels)
    coarse_attention = run_rows(coarse_query, coarse_scale.astype(jnp.int32), coarse_memory[0], coarse_memory[1], coarse_scale.astype(jnp.int32))
    fine_mixed = jnp.dot(fine_attention, out_weight, preferred_element_type=jnp.float32).astype(jnp.bfloat16)
    coarse_mixed = jnp.dot(coarse_attention, out_weight, preferred_element_type=jnp.float32).astype(jnp.bfloat16)
    return fine_mixed, coarse_mixed
```

```python
import functools
import math

import jax
import jax.numpy as jnp
from jax import lax
from jax.experimental import pallas as pl
from jax.experimental.pallas import tpu as pltpu
from jax.sharding import PartitionSpec as P

HD = 128
MASKED = -1e30
LOG2E = math.log2(math.e)
MESH = pl.DeviceIdType.MESH
PAIR, CORES = 2, 2
TILE = 512


def line_is_outer(mesh):
    chips = mesh.devices.reshape(mesh.devices.shape[0], -1)[::CORES, 0]
    try:
        places = [tuple(chip.coords) for chip in chips]
    except (AttributeError, TypeError):
        return True
    fast = [i for i in range(3) if places[0][i] != places[1][i]]
    run = 1
    while run < len(places) and all(
        places[run][i] == places[0][i] for i in range(3) if i not in fast
    ):
        run += 1
    return run == PAIR or len(places) != PAIR * run


def split_queries(rows):
    scaled = rows.astype(jnp.float32) * (HD ** (-0.5) * LOG2E)
    high = scaled.astype(jnp.bfloat16)
    low = (scaled - high.astype(jnp.float32)).astype(jnp.bfloat16)
    return jnp.concatenate([high, low], axis=1)


def scores_of(keys, pair):
    doubled = jnp.concatenate([keys, keys], axis=1)
    return lax.dot_general(
        doubled, pair, (((1,), (1,)), ((), ())), preferred_element_type=jnp.float32
    )


def fold(state, scores, values_t):
    highest, total, weighted = state
    new = jnp.maximum(highest, jnp.max(scores, axis=0, keepdims=True))
    rescale = jnp.exp2(highest - new)
    shifted = jnp.exp2(scores - new)
    total = total * rescale + jnp.sum(shifted, axis=0, keepdims=True)
    weighted = weighted * rescale + jnp.dot(
        values_t, shifted.astype(jnp.bfloat16), preferred_element_type=jnp.float32
    )
    return (new, total, weighted)


def columns_of(head):
    return pl.ds(pl.multiple_of(head * HD, HD), HD)


def schedule_of(line, pieces):
    coarse = [(d, 0) for d in range(1, line)]
    fine = [(d, p) for d in range(1, line) for p in range(1, pieces)]
    takes, rest = [coarse[0]], coarse[1:]
    while rest or fine:
        if rest:
            takes.append(rest.pop(0))
        if fine:
            takes.append(fine.pop(0))
    own = [(0, p) for p in range(pieces)]
    uses = own[:2] + takes[:1] + own[2:] + takes[1:]
    steps = [("O", u) for u in own[:2]] + [("T", takes[0])] + [("O", u) for u in own[2:]]
    steps += [("U", u) for u in uses[:2]]
    takes, uses = takes[1:], uses[2:]
    for count in [2, 2] + [1] * len(takes):
        steps += [("T", u) for u in takes[:count]]
        takes = takes[count:]
        for u in uses[: count if len(steps) < 12 else 1]:
            steps.append(("U", u))
        uses = uses[count if len(steps) < 12 else 1 :]
    steps += [("T", u) for u in takes] + [("U", u) for u in uses]
    order, done = [], False
    for at, step in enumerate(steps):
        order.append(step)
        if step == ("U", (line - 1, 0)):
            order.append(("C", None))
    return order


def kernel(
    line, outer, heads_axis, ratio,
    fq_hbm, cq_hbm, fm_hbm, cm_hbm, lev_hbm, w_hbm,
    fo_hbm, co_hbm,
    kv, lev, klev, fq, cq, fpair, cpair, vt, facc, fstat, cacc, cstat,
    fatt, catt, w, fmine, cmine, fsend, csend, frecv, crecv, fout, cout,
    zr, zs, yr, ys, cr, cs, hs, hr, loc, outs,
):
    keys = cm_hbm.shape[1]
    pieces = 1 + fm_hbm.shape[1] // keys
    groups = kv.shape[3] // HD
    rows, crows = fq.shape[0], cq.shape[0]
    unit = PAIR * CORES * keys
    part, cpart = rows // heads_axis, crows // heads_axis
    width = w.shape[1]
    tiles = width // TILE

    me, head = lax.axis_index("ctx"), lax.axis_index("head")
    core = lax.rem(me, CORES)
    if outer:
        pair, place = lax.rem(me // CORES, PAIR), me // (CORES * PAIR)
    else:
        pair, place = me // (CORES * line), lax.rem(me // CORES, line)

    def device(l, q, c):
        index = (l * PAIR + q) * CORES + c if outer else (q * line + l) * CORES + c
        return (index, head)

    def slot(l, q, c):
        return (l * PAIR + q) * CORES + c

    def span(l, q, c):
        return pl.ds(pl.multiple_of(slot(l, q, c) * keys, keys), keys)

    right, left = device(place + 1, pair, core), device(place - 1, pair, core)
    across, beside = device(place, 1 - pair, core), device(place, pair, 1 - core)
    has_right, has_left = place + 1 < line, place > 0
    others = [lax.rem(head + k, heads_axis) for k in range(1, heads_axis)]

    def greet(target):
        pl.semaphore_signal(barrier, inc=1, device_id=target, device_id_type=MESH)

    barrier = pltpu.get_barrier_semaphore()
    pl.when(has_right)(lambda: greet(right))
    pl.when(has_left)(lambda: greet(left))
    greet(across)
    greet(beside)
    for other in others:
        greet((me, other))

    def held(l, q, c, p):
        if p == pieces:
            return lev.at[slot(l, q, c)]
        return kv.at[p, :, span(l, q, c), :]

    def own_source(p):
        if p == pieces:
            return lev_hbm
        if p == 0:
            return cm_hbm
        return fm_hbm.at[:, (p - 1) * keys : p * keys, :]

    def along(p):
        return [p, pieces] if p == 0 else [p]

    own_copies = [
        pltpu.make_async_copy(own_source(p), held(place, pair, core, p), loc.at[p])
        for p in range(pieces + 1)
    ]
    q_copies = [
        pltpu.make_async_copy(fq_hbm, fq, loc.at[pieces + 1]),
        pltpu.make_async_copy(cq_hbm, cq, loc.at[pieces + 2]),
    ]
    w_copy = pltpu.make_async_copy(w_hbm, w, loc.at[pieces + 3])
    for copy in q_copies + own_copies:
        copy.start()

    def remote(source, l, q, c, p, send, recv, target):
        return pltpu.make_async_remote_copy(
            src_ref=source,
            dst_ref=held(l, q, c, p),
            send_sem=send,
            recv_sem=recv,
            device_id=target,
            device_id_type=MESH,
        )

    def to_line(l, p, way, target, source=None):
        source = held(l, pair, core, p) if source is None else source
        return remote(source, l, pair, core, p, zs.at[way, l, p], zr.at[l, p], target)

    def to_pair(l, p, source=None):
        source = held(l, pair, core, p) if source is None else source
        return remote(source, l, pair, core, p, ys.at[l, p], yr.at[l, p], across)

    def to_core(l, q, p, source=None):
        source = held(l, q, core, p) if source is None else source
        return remote(source, l, q, core, p, cs.at[l, q, p], cr.at[l, q, p], beside)

    def from_line(l, p):
        return remote(
            held(l, pair, core, p), l, pair, core, p, zs.at[0, l, p], zr.at[l, p], across
        )

    def from_pair(l, p):
        at = held(l, 1 - pair, core, p)
        return remote(at, l, 1 - pair, core, p, ys.at[l, p], yr.at[l, p], across)

    def from_core(l, q, p):
        at = held(l, q, 1 - core, p)
        return remote(at, l, q, 1 - core, p, cs.at[l, q, p], cr.at[l, q, p], beside)

    def send_own(p):
        for a in along(p):
            source = own_source(a)
            pl.when(has_right)(lambda: to_line(place, a, 0, right, source).start())
            pl.when(has_left)(lambda: to_line(place, a, 1, left, source).start())
            to_pair(place, a, source).start()
            to_core(place, pair, a, source).start()

    def sides(d):
        if d == 0:
            return [(place, None, None)]
        return [(place - d, place >= d, 0), (place + d, place + d < line, 1)]

    def take_line(d, p):
        for l, valid, way in sides(d):
            onward = has_right if way == 0 else has_left

            @pl.when(valid)
            def _():
                for a in along(p):
                    from_line(l, a).wait_recv()
                    target = right if way == 0 else left
                    pl.when(onward)(lambda: to_line(l, a, way, target).start())
                    to_pair(l, a).start()
                    to_core(l, pair, a).start()

    def take_pair(l, p):
        for a in along(p):
            from_pair(l, a).wait_recv()
            to_core(l, 1 - pair, a).start()

    def step(pair_ref, acc_ref, stat_ref, at, scores, values_t):
        stat = stat_ref[at]
        new, total, weighted = fold((stat[0:1], stat[1:2], acc_ref[at]), scores, values_t)
        stat_ref[at, 0:1] = new
        stat_ref[at, 1:2] = total
        acc_ref[at] = weighted

    cstack = cpair.shape[1] // crows

    def use(l, p):
        base = pl.multiple_of(l * unit, unit)

        @pl.loop(0, groups)
        def _(g):
            vt[...] = kv[p, 1, pl.ds(base, unit), columns_of(g)].T

            @pl.loop(0, ratio // 2)
            def _(h):
                block = kv[p, 0, pl.ds(base, unit), columns_of(g)]
                ats = [g * ratio + h * 2 + k for k in range(2)]
                scores = [scores_of(block, fpair[at]) for at in ats]
                for at, score in zip(ats, scores):
                    step(fpair, facc, fstat, at, score, vt[...])

            if p == 0:
                @pl.loop(0, ratio // cstack)
                def _(h):
                    block = kv[p, 0, pl.ds(base, unit), columns_of(g)]
                    at = g * (ratio // cstack) + h
                    level = klev[pl.ds(base, unit), :]
                    mine = jnp.max(lev[slot(place, pair, core)], axis=0, keepdims=True)
                    allowed = jnp.concatenate([level <= mine] * cstack, axis=1)
                    scores = jnp.where(allowed, scores_of(block, cpair[at]), MASKED)
                    step(cpair, cacc, cstat, at, scores, vt[...])

    def take(d, p):
        if d == 0:
            own_copies[p].wait()
            if p == 0:
                own_copies[pieces].wait()
        for l, valid, way in sides(d):

            def body():
                take_pair(l, p)
                for a in along(p):
                    for q in range(PAIR):
                        from_core(l, q, a).wait_recv()
                if p == 0:
                    for q in range(PAIR):
                        for c in range(CORES):
                            column = lev[slot(l, q, c)].T[:, 0:1]
                            klev[span(l, q, c), :] = jnp.broadcast_to(column, (keys, crows))

            if valid is None:
                body()
            else:
                pl.when(valid)(body)

        if d == 0:
            use(place, p)
        else:

            @pl.loop(0, 2)
            def _(way):
                l = place + (2 * way - 1) * d

                @pl.when(jnp.logical_and(l >= 0, l < line))
                def _():
                    use(l, p)

    def finish(acc, stat):
        return (acc / stat[1:2]).T.astype(jnp.bfloat16)

    def rotated(block):
        return lax.rem(block + heads_axis - head, heads_axis)

    def finish_coarse():
        @pl.loop(0, groups * ratio // cstack)
        def _(at):
            result = finish(cacc[at], cstat[at])
            for k in range(cstack):
                for b in range(heads_axis):
                    to = pl.multiple_of(rotated(b) * cpart, cpart)
                    lo = k * crows + b * cpart
                    catt[pl.ds(to, cpart), columns_of(at * cstack + k)] = result[lo : lo + cpart]

    def finish_fine():
        @pl.loop(0, groups * ratio)
        def _(at):
            result = finish(facc[at], fstat[at])
            for b in range(heads_axis):
                to = pl.multiple_of(rotated(b) * part, part)
                fatt[pl.ds(to, part), columns_of(at)] = result[b * part : (b + 1) * part]

    def share(which, k, t):
        size, send, recv = ((part, fsend, frecv), (cpart, csend, crecv))[which]
        return pltpu.make_async_remote_copy(
            src_ref=send.at[k, t],
            dst_ref=recv.at[k, t],
            send_sem=hs.at[which, k, t],
            recv_sem=hr.at[which, k, t],
            device_id=(me, others[k]),
            device_id_type=MESH,
        )

    def project(which):
        att, mine, send, size = ((fatt, fmine, fsend, part), (catt, cmine, csend, cpart))[which]

        @pl.loop(0, tiles)
        def _(t):
            piece = w[:, pl.ds(pl.multiple_of(t * TILE, TILE), TILE)]
            result = jnp.dot(att[...], piece, preferred_element_type=jnp.float32)
            mine[t] = result[:size]
            for k in range(heads_axis - 1):
                send[k, t] = result[(k + 1) * size : (k + 2) * size].astype(jnp.bfloat16)

            @pl.when(t > 0)
            def _():
                for k in range(heads_axis - 1):
                    share(which, k, t - 1).start()

        for k in range(heads_axis - 1):
            share(which, k, tiles - 1).start()

    def collect(which):
        mine, recv, out, out_hbm = ((fmine, frecv, fout, fo_hbm), (cmine, crecv, cout, co_hbm))[which]

        def put(t):
            at = pl.ds(pl.multiple_of(t * TILE, TILE), TILE)
            return pltpu.make_async_copy(out.at[t], out_hbm.at[:, at], outs.at[which, t])

        @pl.loop(0, tiles)
        def _(t):
            total = mine[t]
            for k in range(heads_axis - 1):
                share(which, k, t).wait_recv()
                total = total + recv[k, t].astype(jnp.float32)
            out[t] = total.astype(jnp.bfloat16)
            put(t).start()

        return put

    facc[...] = jnp.zeros_like(facc)
    cacc[...] = jnp.zeros_like(cacc)
    fstat[...] = jnp.zeros_like(fstat)
    cstat[...] = jnp.zeros_like(cstat)
    fstat[:, 0:1] = jnp.full((fstat.shape[0], 1, fstat.shape[2]), MASKED, jnp.float32)
    cstat[:, 0:1] = jnp.full((cstat.shape[0], 1, cstat.shape[2]), MASKED, jnp.float32)

    greeted = 2 + len(others) + jnp.where(has_right, 1, 0) + jnp.where(has_left, 1, 0)
    pl.semaphore_wait(barrier, greeted)

    first = True
    for kind, which in schedule_of(line, pieces):
        if kind == "O":
            send_own(which[1])
        elif kind == "T":
            take_line(*which)
        elif kind == "U":
            if first:
                w_copy.start()
                for copy in q_copies:
                    copy.wait()

                @pl.loop(0, groups * ratio)
                def _(at):
                    fpair[at] = split_queries(fq[:, columns_of(at)])

                @pl.loop(0, groups * ratio // cstack)
                def _(at):
                    for k in range(cstack):
                        cpair[at, k * crows : (k + 1) * crows] = split_queries(
                            cq[:, columns_of(at * cstack + k)]
                        )

                first = False
            take(*which)
        else:
            finish_coarse()
            w_copy.wait()
            project(1)

    finish_fine()
    project(0)
    cput = collect(1)
    fput = collect(0)

    def done_line(l, way, onward):
        @pl.when(onward)
        def _():
            for a in range(pieces + 1):
                to_line(l, a, way, right if way == 0 else left).wait_send()

    for l in range(line):
        done_line(l, 0, jnp.logical_and(l <= place, has_right))
        done_line(l, 1, jnp.logical_and(l >= place, has_left))
        for a in range(pieces + 1):
            to_pair(l, a).wait_send()
            for q in range(PAIR):
                to_core(l, q, a).wait_send()

    @pl.loop(0, tiles)
    def _(t):
        for k in range(heads_axis - 1):
            share(0, k, t).wait_send()
            share(1, k, t).wait_send()
        cput(t).wait()
        fput(t).wait()


def per_device(mesh_shape, outer, fine_query, fine_memory, coarse_query, coarse_memory, coarse_scale, out_weight):
    heads_axis = mesh_shape["head"]
    line = mesh_shape["ctx"] // (PAIR * CORES)
    rows, width = fine_query.shape
    crows, keys = coarse_query.shape[0], coarse_memory.shape[1]
    groups = coarse_memory.shape[2] // HD
    heads = width // HD
    ratio = heads // groups
    pieces = 1 + fine_memory.shape[1] // keys
    slots = line * PAIR * CORES
    columns = out_weight.shape[1]
    tiles = columns // TILE
    cstack = 2
    part, cpart = rows // heads_axis, crows // heads_axis
    levels = jnp.broadcast_to(coarse_scale.astype(jnp.float32)[None, :], (8, keys))
    f32, bf16 = jnp.float32, jnp.bfloat16
    anywhere = pl.BlockSpec(memory_space=pl.ANY)
    pairs = rows * slots * keys * pieces * heads + crows * slots * keys * heads
    return pl.pallas_call(
        functools.partial(kernel, line, outer, heads_axis, ratio),
        out_shape=(
            jax.ShapeDtypeStruct((part, columns), bf16),
            jax.ShapeDtypeStruct((cpart, columns), bf16),
        ),
        in_specs=[anywhere] * 6,
        out_specs=(anywhere, anywhere),
        scratch_shapes=[
            pltpu.VMEM((pieces, 2, slots * keys, groups * HD), bf16),
            pltpu.VMEM((slots, 8, keys), f32),
            pltpu.VMEM((slots * keys, crows), f32),
            pltpu.VMEM((rows, width), bf16),
            pltpu.VMEM((crows, width), bf16),
            pltpu.VMEM((heads, rows, 2 * HD), bf16),
            pltpu.VMEM((heads // cstack, cstack * crows, 2 * HD), bf16),
            pltpu.VMEM((HD, PAIR * CORES * keys), bf16),
            pltpu.VMEM((heads, HD, rows), f32),
            pltpu.VMEM((heads, 8, rows), f32),
            pltpu.VMEM((heads // cstack, HD, cstack * crows), f32),
            pltpu.VMEM((heads // cstack, 8, cstack * crows), f32),
            pltpu.VMEM((rows, width), bf16),
            pltpu.VMEM((crows, width), bf16),
            pltpu.VMEM(out_weight.shape, bf16),
            pltpu.VMEM((tiles, part, TILE), f32),
            pltpu.VMEM((tiles, cpart, TILE), f32),
            pltpu.VMEM((heads_axis - 1, tiles, part, TILE), bf16),
            pltpu.VMEM((heads_axis - 1, tiles, cpart, TILE), bf16),
            pltpu.VMEM((heads_axis - 1, tiles, part, TILE), bf16),
            pltpu.VMEM((heads_axis - 1, tiles, cpart, TILE), bf16),
            pltpu.VMEM((tiles, part, TILE), bf16),
            pltpu.VMEM((tiles, cpart, TILE), bf16),
            pltpu.SemaphoreType.DMA((line, pieces + 1)),
            pltpu.SemaphoreType.DMA((2, line, pieces + 1)),
            pltpu.SemaphoreType.DMA((line, pieces + 1)),
            pltpu.SemaphoreType.DMA((line, pieces + 1)),
            pltpu.SemaphoreType.DMA((line, PAIR, pieces + 1)),
            pltpu.SemaphoreType.DMA((line, PAIR, pieces + 1)),
            pltpu.SemaphoreType.DMA((2, heads_axis - 1, tiles)),
            pltpu.SemaphoreType.DMA((2, heads_axis - 1, tiles)),
            pltpu.SemaphoreType.DMA((pieces + 4,)),
            pltpu.SemaphoreType.DMA((2, tiles)),
        ],
        compiler_params=pltpu.CompilerParams(
            collective_id=0, has_side_effects=True, vmem_limit_bytes=62 << 20
        ),
        cost_estimate=pl.CostEstimate(
            flops=8 * pairs * HD, transcendentals=pairs, bytes_accessed=4 * rows * width
        ),
    )(fine_query, coarse_query, fine_memory, coarse_memory, levels, out_weight)


def solution(mesh):
    placed = (
        P("ctx", "head"),
        P(None, "ctx", "head"),
        P("ctx", "head"),
        P(None, "ctx", "head"),
        P("ctx"),
        P("head", None),
    )
    return jax.shard_map(
        functools.partial(per_device, dict(mesh.shape), line_is_outer(mesh)),
        mesh=mesh,
        in_specs=placed,
        out_specs=(P(("ctx", "head"), None), P(("ctx", "head"), None)),
        check_vma=False,
    )
```
